32 devices in a mesh: row: 8 (over z, core), col: 4 (over y, x).
Axes of the slice: x: 2, y: 2, z: 4, core: 2. Of those that a mesh axis runs over, the one named last changes fastest.
Arguments:
- rhs: bfloat16 [3, 8, 64, 256], P(None, 'row'), may hold values from -6 to 6
- dinv: bfloat16 [3, 8, 256, 256], P(None, 'row'), as said below
- tiles: bfloat16 [2, 8, 8, 256, 256], P(None, 'row', 'col'), may hold values from -0.09375 to 0.09375
- pattern: int32 [2, 2, 8, 8], P(None, None, 'row', 'col'), may hold values from 0 to 7, as said below
Outputs:
- solution: float32 [3, 8, 64, 256], P(None, 'row')
The draws below stay inside these ranges and needn't reach their ends.
Inputs may be any that keep to these rules, and one draw needn't show every extreme that they name: pattern[0, l, p, t] = p; pattern[1, l, p, t] = j has (j) modulo the size of col equal to t // 2; positions may repeat, and repeated tiles add. `dinv`: lower triangular with a positive diagonal.
All inputs are finite; a program needn't handle non-finite values.
Results may differ from the reference program's by a relative error of at most 0.0055.
Values may be sent and summed in bfloat16 or wider, within the bound.
No kernel may reach another device: no remote copies, remote signals or barrier semaphores. Data moves between devices by JAX's collectives and lax.ppermute only.
A program may use at most 64 MiB of HBM per device.

```python
import math
import jax
import jax.numpy as jnp
from jax import lax

BS = 256
NRHS = 64
LEVELS = 3
ROWS_DEV = 1
SLOTS = 2
N_ROW = 8
N_COL = 4


def draw_dinv(key, part):
    key_diag, key_off = jax.random.split(jax.random.fold_in(key, 3))
    block_rows = ROWS_DEV * N_ROW
    array_shape = (LEVELS, block_rows, BS, BS)
    diagonal = jnp.exp(jax.random.uniform(key_diag, (LEVELS, block_rows, BS), jnp.float32, math.log(0.5), math.log(2.0)))
    lower = jax.random.normal(key_off, array_shape, jnp.float32) * (0.5 / math.sqrt(BS))
    row_ids = jnp.arange(BS, dtype=jnp.int32)[:, None]
    col_ids = jnp.arange(BS, dtype=jnp.int32)[None, :]
    strict = (col_ids < row_ids).astype(jnp.float32)
    identity = (col_ids == row_ids).astype(jnp.float32)
    matrix = lower * strict + identity * diagonal[..., None]
    return matrix.astype(jnp.bfloat16)


def draw_pattern(key, part):
    key_row, key_group, key_col = jax.random.split(jax.random.fold_in(key, 11), 3)
    array_shape = (LEVELS - 1, N_ROW, N_COL * SLOTS)
    block_rows = ROWS_DEV * N_ROW
    device_row = jnp.arange(N_ROW, dtype=jnp.int32)[None, :, None]
    device_col = (jnp.arange(N_COL * SLOTS, dtype=jnp.int32) // SLOTS)[None, None, :]
    row_offset = jax.random.randint(key_row, array_shape, 0, ROWS_DEV)
    group_pick = jax.random.randint(key_group, array_shape, 0, N_ROW // N_COL)
    col_offset = jax.random.randint(key_col, array_shape, 0, ROWS_DEV)
    row_values = device_row * ROWS_DEV + row_offset
    col_values = (device_col + N_COL * group_pick) * ROWS_DEV + col_offset
    row_values = row_values.at[0, 0, 0].set(0).at[0, N_ROW - 1, 0].set(block_rows - 1)
    col_values = col_values.at[0, 0, 0].set(0).at[0, 0, N_COL * SLOTS - 1].set(block_rows - 1)
    return jnp.stack([row_values, col_values]).astype(jnp.int32)


def block_levels(key, dims, pieces, low, largest):
    def one(position, shards_of):
        draws = jax.random.uniform(jax.random.fold_in(jax.random.fold_in(key, 6), position), (shards_of,), jnp.float32, low / len(pieces), largest / len(pieces))
        return jnp.repeat(jnp.exp(draws), dims[position] // shards_of).reshape((-1,) + (1,) * (len(dims) - position - 1))

    level = one(*pieces[0])
    for cut in pieces[1:]:
        level = level * one(*cut)
    return level


def gaussian(rng, shape, scale, reach, shards=(), kind=jnp.bfloat16):
    array = scale * jax.random.normal(rng, shape, jnp.float32)
    if shards:
        array = array * block_levels(rng, shape, shards, -0.22, 0.18)
    return jnp.clip(array, -reach, reach).astype(kind)


def setup_inputs(seed: int = 0) -> dict:
    seeds = jax.random.split(jax.random.key(seed), 5)
    rhs = gaussian(seeds[0], (LEVELS, ROWS_DEV * N_ROW, NRHS, BS), 1.0, 6.0, ((1, 8),))
    dinv = draw_dinv(jax.random.fold_in(seeds[4], 71), 0)
    tiles = gaussian(seeds[2], (LEVELS - 1, N_ROW, N_COL * SLOTS, BS, BS), (2 * BS * SLOTS * N_COL // ROWS_DEV) ** -0.5, 0.09375, ((1, 8), (2, 4)))
    pattern = draw_pattern(jax.random.fold_in(seeds[4], 71), 0)
    return {"rhs": rhs, "dinv": dinv, "tiles": tiles, "pattern": pattern}


def reference(rhs, dinv, tiles, pattern):
    block_rows = ROWS_DEV * N_ROW
    row_index = pattern[0].reshape(LEVELS - 1, -1)
    col_index = pattern[1].reshape(LEVELS - 1, -1)
    factor_tiles = tiles.reshape(LEVELS - 1, -1, BS, BS)
    forward_list = []
    previous = None
    for level_now in range(LEVELS):
        current = rhs[level_now].astype(jnp.float32)
        if level_now > 0:
            source = previous[col_index[level_now - 1]].astype(jnp.float32)
            product = jnp.einsum("mjb,mab->mja", source, factor_tiles[level_now - 1].astype(jnp.float32), precision=lax.Precision.HIGHEST)
            updates = jnp.zeros((block_rows, NRHS, BS), jnp.float32).at[row_index[level_now - 1]].add(product)
            current = current - updates
        rounded = lax.optimization_barrier(current.astype(jnp.bfloat16)).astype(jnp.float32)
        solved = jnp.einsum("wjb,wab->wja", rounded, dinv[level_now].astype(jnp.float32), precision=lax.Precision.HIGHEST)
        forward_list.append(solved)
        previous = solved.astype(jnp.bfloat16)
    backward_list = [None] * LEVELS
    following = None
    for level_now in range(LEVELS - 1, -1, -1):
        remainder = forward_list[level_now]
        if level_now < LEVELS - 1:
            source = following[row_index[level_now]].astype(jnp.float32)
            product = jnp.einsum("mja,mab->mjb", source, factor_tiles[level_now].astype(jnp.float32), precision=lax.Precision.HIGHEST)
            updates = jnp.zeros((block_rows, NRHS, BS), jnp.float32).at[col_index[level_now]].add(product)
            remainder = remainder - updates
        rounded = lax.optimization_barrier(remainder.astype(jnp.bfloat16)).astype(jnp.float32)
        solved = jnp.einsum("wjb,wba->wja", rounded, dinv[level_now].astype(jnp.float32), precision=lax.Precision.HIGHEST)
        backward_list[level_now] = solved
        following = solved.astype(jnp.bfloat16)
    return jnp.stack(backward_list)
```

```python
import functools

import jax
import jax.numpy as jnp
from jax import lax
from jax.experimental import pallas as pl
from jax.experimental.pallas import tpu as pltpu
from jax.sharding import PartitionSpec as P

F32 = jnp.float32
BF16 = jnp.bfloat16


def swap(value, axis, size, mask):
    return lax.ppermute(value, axis, [(i, i ^ mask) for i in range(size)])


def dot_t(a, b):
    return lax.dot_general(a, b, (((1,), (1,)), ((), ())), preferred_element_type=F32)


def dot_n(a, b):
    return lax.dot_general(a, b, (((1,), (0,)), ((), ())), preferred_element_type=F32)


def update(near, far, tile_refs, repeat):
    cols = len(tile_refs)
    row = lax.axis_index("row")
    col = lax.axis_index("col")
    total = None
    for step, tile_ref in enumerate(tile_refs):
        for group in range(repeat):
            place = row ^ ((col ^ step) + cols * group)
            offset = place // 2
            odd = jnp.broadcast_to(place % 2, near.shape[1:]) == 1
            segment = jnp.where(odd, far[offset], near[offset])
            term = dot_t(segment, tile_ref[group])
            total = term if total is None else total + term
    return total


def spread(solved, tile_refs, repeat, parts, keep_ref, send_ref):
    cols = len(tile_refs)
    row = lax.axis_index("row")
    col = lax.axis_index("col")
    for step, tile_ref in enumerate(tile_refs):
        for group in range(repeat):
            place = row ^ ((col ^ step) + cols * group)
            parts[place % 2, place // 2] = dot_n(solved, tile_ref[group])
    keep_ref[...] = parts[0]
    send_ref[...] = parts[1].astype(BF16)


def first_kernel(rhs, dinv, out, out_b):
    solved = dot_t(rhs[...], dinv[...])
    out[...] = solved
    out_b[...] = solved.astype(BF16)


def forward_kernel(repeat, cols, near, far, *refs):
    tile_refs, (rhs, dinv, out, out_b) = refs[:cols], refs[cols:]
    current = rhs[...].astype(F32) - update(near, far, tile_refs, repeat)
    solved = dot_t(current.astype(BF16), dinv[...])
    out[...] = solved
    out_b[...] = solved.astype(BF16)


def turn_kernel(repeat, cols, near, far, *refs):
    tile_refs, (rhs, dinv, out, keep, send, parts) = refs[:cols], refs[cols:]
    current = rhs[...].astype(F32) - update(near, far, tile_refs, repeat)
    forward = dot_t(current.astype(BF16), dinv[...])
    solved = dot_n(forward.astype(BF16), dinv[...])
    out[...] = solved
    spread(solved.astype(BF16), tile_refs, repeat, parts, keep, send)


def remainder(count, refs):
    total = refs[0][...].astype(F32)
    for ref in refs[1:count]:
        total = total + ref[...].astype(F32)
    return total


def backward_kernel(repeat, cols, count, *refs):
    arrived, tile_refs = refs[:count], refs[count : count + cols]
    forward, dinv, out, keep, send, parts = refs[count + cols :]
    rest = forward[...] - remainder(count, arrived)
    solved = dot_n(rest.astype(BF16), dinv[...])
    out[...] = solved
    spread(solved.astype(BF16), tile_refs, repeat, parts, keep, send)


def last_kernel(count, upper_count, *refs):
    arrived = refs[:count]
    forward, dinv = refs[count : count + 2]
    upper = refs[count + 2 : count + 2 + upper_count]
    out = refs[-1]
    rest = forward[...] - remainder(count, arrived)
    out[0, 0] = dot_n(rest.astype(BF16), dinv[...])
    for index, ref in enumerate(upper):
        out[index + 1, 0] = ref[...]


def call(kernel, outs, scratch, *args):
    return pl.pallas_call(
        kernel,
        out_shape=outs,
        in_specs=[pl.BlockSpec(memory_space=pltpu.VMEM)] * len(args),
        out_specs=jax.tree.map(lambda _: pl.BlockSpec(memory_space=pltpu.VMEM), outs),
        scratch_shapes=scratch,
    )(*args)


def per_device(rhs, dinv, tiles, pattern):
    levels, blocks, nrhs, bs = rhs.shape
    assert blocks == 1
    cols = lax.axis_size("col")
    rows = lax.axis_size("row")
    repeat = rows // cols
    chips = rows // 2
    slots = pattern[1, :, 0, :] // cols

    seg = jax.ShapeDtypeStruct((nrhs, bs), F32)
    seg_b = jax.ShapeDtypeStruct((nrhs, bs), BF16)
    chip_segs = jax.ShapeDtypeStruct((chips, nrhs, bs), F32)
    chip_segs_b = jax.ShapeDtypeStruct((chips, nrhs, bs), BF16)
    parts = [pltpu.VMEM((2, chips, nrhs, bs), F32)]

    def gathered_tiles(level):
        picks = (slots[level][None, :] == jnp.arange(repeat, dtype=jnp.int32)[:, None]).astype(F32)
        own = jnp.sum(picks[:, :, None, None] * tiles[level, 0][None].astype(F32), axis=1).astype(BF16)
        return [own] + [swap(own, "col", cols, step) for step in range(1, cols)]

    def gather(mine):
        near = [mine] + [swap(mine, "row", rows, 2 * chip) for chip in range(1, chips)]
        near = jnp.stack(near)
        return near, swap(near, "row", rows, 1)

    def scatter(keep, send):
        total = keep + swap(send, "row", rows, 1).astype(F32)
        return [total[0]] + [
            swap(total[chip].astype(BF16), "row", rows, 2 * chip) for chip in range(1, chips)
        ]

    level_tiles = [gathered_tiles(level) for level in range(levels - 1)]
    forward, mine = call(first_kernel, (seg, seg_b), [], rhs[0, 0], dinv[0, 0])
    forwards = [forward]
    for level in range(1, levels - 1):
        near, far = gather(mine)
        forward, mine = call(
            functools.partial(forward_kernel, repeat, cols),
            (seg, seg_b), [], near, far, *level_tiles[level - 1], rhs[level, 0], dinv[level, 0],
        )
        forwards.append(forward)
    near, far = gather(mine)
    top = levels - 1
    solved, keep, send = call(
        functools.partial(turn_kernel, repeat, cols),
        (seg, chip_segs, chip_segs_b), parts, near, far, *level_tiles[top - 1], rhs[top, 0], dinv[top, 0],
    )
    upper = [solved]
    for level in range(levels - 2, 0, -1):
        arrived = scatter(keep, send)
        solved, keep, send = call(
            functools.partial(backward_kernel, repeat, cols, chips),
            (seg, chip_segs, chip_segs_b), parts, *arrived, *level_tiles[level - 1], forwards[level], dinv[level, 0],
        )
        upper.insert(0, solved)
    arrived = scatter(keep, send)
    return call(
        functools.partial(last_kernel, chips, len(upper)),
        jax.ShapeDtypeStruct(rhs.shape, F32), [], *arrived, forwards[0], dinv[0, 0], *upper,
    )


def solution(mesh):
    in_specs = (
        P(None, "row", None, None),
        P(None, "row", None, None),
        P(None, "row", "col", None, None),
        P(None, None, "row", "col"),
    )
    out_specs = P(None, "row", None, None)
    return jax.shard_map(
        per_device, mesh=mesh, in_specs=in_specs, out_specs=out_specs, check_vma=False
    )
```

```python
import functools

import jax
import jax.numpy as jnp
from jax import lax
from jax.experimental import pallas as pl
from jax.experimental.pallas import tpu as pltpu
from jax.sharding import PartitionSpec as P


F32 = jnp.float32
BF16 = jnp.bfloat16
VMEM_LIMIT = 16 * 2**20
FIRST_LIMIT = int(62 * 2**20)


def send_order(cols):
    return sorted(range(1, cols), key=lambda step: (step & 1 == 0, -step))


def swap(value, axis, size, mask):
    return lax.ppermute(value, axis, [(i, i ^ mask) for i in range(size)])


def dot_t(a, b):
    return lax.dot_general(a, b, (((1,), (1,)), ((), ())), preferred_element_type=F32)


def dot_n(a, b):
    return lax.dot_general(a, b, (((1,), (0,)), ((), ())), preferred_element_type=F32)


def update(near, far, tile_refs, repeat):
    cols = len(tile_refs)
    row = lax.axis_index("row")
    col = lax.axis_index("col")
    total = None
    for step, tile_ref in enumerate(tile_refs):
        for group in range(repeat):
            place = row ^ ((col ^ step) + cols * group)
            offset = place // 2
            odd = jnp.broadcast_to(place % 2, near.shape[1:]) == 1
            segment = jnp.where(odd, far[offset], near[offset])
            term = dot_t(segment, tile_ref[group])
            total = term if total is None else total + term
    return total


def spread(solved, tile_refs, repeat, parts, keep_ref, send_ref):
    cols = len(tile_refs)
    row = lax.axis_index("row")
    col = lax.axis_index("col")
    for step, tile_ref in enumerate(tile_refs):
        for group in range(repeat):
            place = row ^ ((col ^ step) + cols * group)
            parts[place % 2, place // 2] = dot_n(solved, tile_ref[group])
    keep_ref[...] = parts[0]
    send_ref[...] = parts[1].astype(BF16)


def first_kernel(cols, pattern, rhs, dinv, tiles, out, out_b, *rest):
    levels = tiles.shape[0]
    owns, (rhs_v, dinv_v, tiles_v, sems) = rest[:levels], rest[levels:]
    pairs = [(rhs.at[0, 0], rhs_v), (dinv.at[0, 0], dinv_v)]
    pairs += [(tiles.at[level, 0], tiles_v.at[level]) for level in range(levels)]
    copies = [
        pltpu.make_async_copy(source, target, sems.at[index])
        for index, (source, target) in enumerate(pairs)
    ]
    for copy in copies:
        copy.start()
    copies[0].wait()
    copies[1].wait()
    solved = dot_t(rhs_v[...], dinv_v[...])
    out[...] = solved
    out_b[...] = solved.astype(BF16)
    for level, own in enumerate(owns):
        copies[2 + level].wait()
        for group in range(own.shape[0]):
            total = jnp.zeros(own.shape[1:], F32)
            for slot in range(tiles_v.shape[1]):
                here = (pattern[1, level, 0, slot] // cols == group).astype(F32)
                total = total + tiles_v[level, slot].astype(F32) * here
            own[group] = total.astype(BF16)


def forward_kernel(level, repeat, cols, near, far, *refs):
    tile_refs, (rhs, dinv, out, out_b) = refs[:cols], refs[cols:]
    current = rhs[level, 0].astype(F32) - update(near, far, tile_refs, repeat)
    solved = dot_t(current.astype(BF16), dinv[level, 0])
    out[...] = solved
    out_b[...] = solved.astype(BF16)


def turn_kernel(level, repeat, cols, near, far, *refs):
    tile_refs, (rhs, dinv, out, keep, send, parts) = refs[:cols], refs[cols:]
    current = rhs[level, 0].astype(F32) - update(near, far, tile_refs, repeat)
    forward = dot_t(current.astype(BF16), dinv[level, 0])
    solved = dot_n(forward.astype(BF16), dinv[level, 0])
    out[...] = solved
    spread(solved.astype(BF16), tile_refs, repeat, parts, keep, send)


def remainder(count, refs):
    total = refs[0][...].astype(F32)
    for ref in refs[1:count]:
        total = total + ref[...].astype(F32)
    return total


def backward_kernel(level, repeat, cols, count, *refs):
    arrived, tile_refs = refs[:count], refs[count : count + cols]
    forward, dinv, out, keep, send, parts = refs[count + cols :]
    rest = forward[...] - remainder(count, arrived)
    solved = dot_n(rest.astype(BF16), dinv[level, 0])
    out[...] = solved
    spread(solved.astype(BF16), tile_refs, repeat, parts, keep, send)


def last_kernel(count, upper_count, *refs):
    arrived = refs[:count]
    forward, dinv = refs[count : count + 2]
    upper = refs[count + 2 : count + 2 + upper_count]
    out = refs[-1]
    rest = forward[...] - remainder(count, arrived)
    out[0, 0] = dot_n(rest.astype(BF16), dinv[0, 0])
    for index, ref in enumerate(upper):
        out[index + 1, 0] = ref[...]


def call(kernel, outs, scratch, *args, scalars=(), space=pltpu.VMEM, limit=VMEM_LIMIT):
    return pl.pallas_call(
        kernel,
        out_shape=outs,
        in_specs=[pl.BlockSpec(memory_space=pltpu.SMEM)] * len(scalars)
        + [pl.BlockSpec(memory_space=space)] * len(args),
        out_specs=jax.tree.map(lambda _: pl.BlockSpec(memory_space=pltpu.VMEM), outs),
        scratch_shapes=scratch,
        compiler_params=pltpu.CompilerParams(vmem_limit_bytes=limit),
    )(*scalars, *args)


def per_device(rhs, dinv, tiles, pattern):
    levels, blocks, nrhs, bs = rhs.shape
    assert blocks == 1
    cols = lax.axis_size("col")
    rows = lax.axis_size("row")
    repeat = rows // cols
    chips = rows // 2

    seg = jax.ShapeDtypeStruct((nrhs, bs), F32)
    seg_b = jax.ShapeDtypeStruct((nrhs, bs), BF16)
    chip_segs = jax.ShapeDtypeStruct((chips, nrhs, bs), F32)
    chip_segs_b = jax.ShapeDtypeStruct((chips, nrhs, bs), BF16)
    parts = [pltpu.VMEM((2, chips, nrhs, bs), F32)]

    def gathered_tiles(own):
        found = [own] + [None] * (cols - 1)
        for step in send_order(cols):
            found[step] = swap(own, "col", cols, step)
        return found

    def gather(mine):
        near = [mine]
        for chip in range(1, chips):
            near.append(swap(mine, "row", rows, 2 * chip))
        near = jnp.stack(near)
        return near, swap(near, "row", rows, 1)

    def scatter(keep, send):
        total = keep + swap(send, "row", rows, 1).astype(F32)
        return [total[0]] + [
            swap(total[chip].astype(BF16), "row", rows, 2 * chip) for chip in range(1, chips)
        ]

    own_tiles = jax.ShapeDtypeStruct((repeat, bs, bs), BF16)
    forward, mine, *owns = call(
        functools.partial(first_kernel, cols),
        (seg, seg_b) + (own_tiles,) * (levels - 1),
        [
            pltpu.VMEM((nrhs, bs), BF16),
            pltpu.VMEM((bs, bs), BF16),
            pltpu.VMEM((levels - 1,) + tiles.shape[2:], BF16),
            pltpu.SemaphoreType.DMA((levels + 1,)),
        ],
        rhs, dinv, tiles, scalars=(pattern,), space=pl.ANY, limit=FIRST_LIMIT,
    )
    level_tiles = [gathered_tiles(own) for own in owns]
    forwards = [forward]
    for level in range(1, levels - 1):
        near, far = gather(mine)
        forward, mine = call(
            functools.partial(forward_kernel, level, repeat, cols),
            (seg, seg_b), [], near, far, *level_tiles[level - 1], rhs, dinv,
        )
        forwards.append(forward)
    top = levels - 1
    near, far = gather(mine)
    solved, keep, send = call(
        functools.partial(turn_kernel, top, repeat, cols),
        (seg, chip_segs, chip_segs_b), parts, near, far, *level_tiles[top - 1], rhs, dinv,
    )
    upper = [solved]
    for level in range(levels - 2, 0, -1):
        arrived = scatter(keep, send)
        solved, keep, send = call(
            functools.partial(backward_kernel, level, repeat, cols, chips),
            (seg, chip_segs, chip_segs_b), parts, *arrived, *level_tiles[level - 1], forwards[level], dinv,
        )
        upper.insert(0, solved)
    arrived = scatter(keep, send)
    return call(
        functools.partial(last_kernel, chips, len(upper)),
        jax.ShapeDtypeStruct(rhs.shape, F32), [], *arrived, forwards[0], dinv, *upper,
    )


def solution(mesh):
    in_specs = (
        P(None, "row", None, None),
        P(None, "row", None, None),
        P(None, "row", "col", None, None),
        P(None, None, "row", "col"),
    )
    out_specs = P(None, "row", None, None)

    return jax.shard_map(
        per_device, mesh=mesh, in_specs=in_specs, out_specs=out_specs, check_vma=False
    )
```

```python
import functools

import jax
import jax.numpy as jnp
from jax import lax
from jax.experimental import pallas as pl
from jax.experimental.pallas import tpu as pltpu
from jax.sharding import PartitionSpec as P


F32 = jnp.float32
BF16 = jnp.bfloat16
VMEM_LIMIT = 16 * 2**20


def send_order(cols):
    return sorted(range(1, cols), key=lambda step: -step)


def swap(value, axis, size, mask):
    return lax.ppermute(value, axis, [(i, i ^ mask) for i in range(size)])


def dot_t(a, b):
    return lax.dot_general(a, b, (((1,), (1,)), ((), ())), preferred_element_type=F32)


def dot_n(a, b):
    return lax.dot_general(a, b, (((1,), (0,)), ((), ())), preferred_element_type=F32)


def update(near, far, tile_refs, steps, repeat, cols):
    row = lax.axis_index("row")
    col = lax.axis_index("col")
    total = None
    for step, tile_ref in zip(steps, tile_refs):
        for group in range(repeat):
            place = row ^ ((col ^ step) + cols * group)
            odd = jnp.broadcast_to(place % 2, near.shape[1:]) == 1
            segment = jnp.where(odd, far[place // 2], near[place // 2])
            term = dot_t(segment, tile_ref[group])
            total = term if total is None else total + term
    return total


def pick(tile_refs, pair, group, first):
    even, odd = tile_refs[2 * pair], tile_refs[2 * pair + 1]
    odd_first = jnp.broadcast_to(first, even.shape[1:]) == 1
    return jnp.where(odd_first, odd[group], even[group])


def spread(solved, parity, tile_refs, repeat, out):
    cols = len(tile_refs)
    row = lax.axis_index("row")
    col = lax.axis_index("col")
    first = (row + col + parity) % 2
    for pair in range(cols // 2):
        for group in range(repeat):
            place = row ^ ((col ^ (2 * pair + first)) + cols * group)
            tile = pick(tile_refs, pair, group, first)
            out[place // 2] = dot_n(solved, tile).astype(out.dtype)


def first_kernel(rhs, dinv, out, out_b):
    solved = dot_t(rhs[0, 0], dinv[0, 0])
    out[...] = solved
    out_b[...] = solved.astype(BF16)


def early_kernel(repeat, cols, steps, near, far, *refs):
    refs[-1][...] = update(near, far, refs[:-1], steps, repeat, cols)


def forward_kernel(level, repeat, cols, steps, part, near, far, *refs):
    tile_refs, (rhs, dinv, out, out_b) = refs[: len(steps)], refs[len(steps) :]
    late = update(near, far, tile_refs, steps, repeat, cols)
    current = rhs[level, 0].astype(F32) - (part[...] + late)
    solved = dot_t(current.astype(BF16), dinv[level, 0])
    out[...] = solved
    out_b[...] = solved.astype(BF16)


def turn_kernel(level, repeat, cols, steps, part, near, far, *refs):
    tile_refs, (rhs, dinv, out, out_b, send) = refs[:cols], refs[cols:]
    late = update(near, far, [tile_refs[step] for step in steps], steps, repeat, cols)
    current = rhs[level, 0].astype(F32) - (part[...] + late)
    forward = dot_t(current.astype(BF16), dinv[level, 0])
    solved = dot_n(forward.astype(BF16), dinv[level, 0])
    out[...] = solved
    solved = solved.astype(BF16)
    out_b[...] = solved
    spread(solved, 1, tile_refs, repeat, send)


def keep_kernel(repeat, solved, *refs):
    spread(solved[...], 0, refs[:-1], repeat, refs[-1])


def remainder(count, refs):
    total = refs[0][...].astype(F32)
    for ref in refs[1:count]:
        total = total + ref[...].astype(F32)
    return total


def backward_kernel(level, repeat, cols, count, *refs):
    arrived, tile_refs = refs[:count], refs[count : count + cols]
    forward, dinv, out, out_b, send = refs[count + cols :]
    rest = forward[...] - remainder(count, arrived)
    solved = dot_n(rest.astype(BF16), dinv[level, 0])
    out[...] = solved
    solved = solved.astype(BF16)
    out_b[...] = solved
    spread(solved, 1, tile_refs, repeat, send)


def last_kernel(count, upper_count, *refs):
    arrived = refs[:count]
    forward, dinv = refs[count : count + 2]
    upper = refs[count + 2 : count + 2 + upper_count]
    out = refs[-1]
    rest = forward[...] - remainder(count, arrived)
    out[0, 0] = dot_n(rest.astype(BF16), dinv[0, 0])
    for index, ref in enumerate(upper):
        out[index + 1, 0] = ref[...]


def call(kernel, outs, scratch, *args):
    return pl.pallas_call(
        kernel,
        out_shape=outs,
        in_specs=[pl.BlockSpec(memory_space=pltpu.VMEM)] * len(args),
        out_specs=jax.tree.map(lambda _: pl.BlockSpec(memory_space=pltpu.VMEM), outs),
        scratch_shapes=scratch,
        compiler_params=pltpu.CompilerParams(vmem_limit_bytes=VMEM_LIMIT),
    )(*args)


def per_device(rhs, dinv, tiles, pattern):
    levels, blocks, nrhs, bs = rhs.shape
    assert blocks == 1
    cols = lax.axis_size("col")
    rows = lax.axis_size("row")
    repeat = rows // cols
    chips = rows // 2

    seg = jax.ShapeDtypeStruct((nrhs, bs), F32)
    seg_b = jax.ShapeDtypeStruct((nrhs, bs), BF16)
    chip_segs = jax.ShapeDtypeStruct((chips, nrhs, bs), F32)
    chip_segs_b = jax.ShapeDtypeStruct((chips, nrhs, bs), BF16)

    def gathered_tiles(level, after):
        groups = jnp.arange(repeat, dtype=jnp.int32)[:, None, None, None]
        raw, slots = tiles[level, 0], pattern[1, level, 0]
        if after is not None:
            raw, slots, _ = lax.optimization_barrier((raw, slots, after))
        here = (slots // cols)[None, :, None, None] == groups
        own = jnp.sum(jnp.where(here, raw[None].astype(F32), 0.0), axis=1).astype(BF16)
        found = [own] + [None] * (cols - 1)
        for step in send_order(cols):
            found[step] = swap(own, "col", cols, step)
        return found

    def gather(mine):
        near = [mine]
        for chip in range(1, chips):
            near.append(swap(mine, "row", rows, 2 * chip))
        near = jnp.stack(near)
        return near, swap(near, "row", rows, 1)

    def scatter(solved, send, found_tiles):
        other = swap(send, "row", rows, 1)
        keep = call(functools.partial(keep_kernel, repeat), chip_segs, [], solved, *found_tiles)
        total = keep + other.astype(F32)
        found = [total[0]]
        for chip in range(1, chips):
            found.append(swap(total[chip].astype(BF16), "row", rows, 2 * chip))
        return found

    late_steps = send_order(cols)[-2:]
    early_steps = [step for step in range(cols) if step not in late_steps]

    def early_part(near, far, found_tiles):
        kernel = functools.partial(early_kernel, repeat, cols, early_steps)
        return call(kernel, seg, [], near, far, *[found_tiles[step] for step in early_steps])

    level_tiles = []
    for level in range(levels - 1):
        level_tiles.append(gathered_tiles(level, level_tiles[-1][0] if level_tiles else None))
    forward, mine = call(first_kernel, (seg, seg_b), [], rhs, dinv)
    forwards = [forward]
    for level in range(1, levels - 1):
        near, far = gather(mine)
        found_tiles = level_tiles[level - 1]
        forward, mine = call(
            functools.partial(forward_kernel, level, repeat, cols, late_steps),
            (seg, seg_b), [], early_part(near, far, found_tiles), near, far,
            *[found_tiles[step] for step in late_steps], rhs, dinv,
        )
        forwards.append(forward)
    top = levels - 1
    near, far = gather(mine)
    found_tiles = level_tiles[top - 1]
    solved, solved_b, send = call(
        functools.partial(turn_kernel, top, repeat, cols, late_steps),
        (seg, seg_b, chip_segs_b), [], early_part(near, far, found_tiles), near, far,
        *found_tiles, rhs, dinv,
    )
    upper = [solved]
    for level in range(levels - 2, 0, -1):
        arrived = scatter(solved_b, send, found_tiles)
        found_tiles = level_tiles[level - 1]
        solved, solved_b, send = call(
            functools.partial(backward_kernel, level, repeat, cols, chips),
            (seg, seg_b, chip_segs_b), [], *arrived, *found_tiles, forwards[level], dinv,
        )
        upper.insert(0, solved)
    arrived = scatter(solved_b, send, found_tiles)
    return call(
        functools.partial(last_kernel, chips, len(upper)),
        jax.ShapeDtypeStruct(rhs.shape, F32), [], *arrived, forwards[0], dinv, *upper,
    )


def solution(mesh):
    in_specs = (
        P(None, "row", None, None),
        P(None, "row", None, None),
        P(None, "row", "col", None, None),
        P(None, None, "row", "col"),
    )
    out_specs = P(None, "row", None, None)

    return jax.shard_map(
        per_device, mesh=mesh, in_specs=in_specs, out_specs=out_specs, check_vma=False
    )
```

```python
import functools

import jax
import jax.numpy as jnp
from jax import lax
from jax.experimental import pallas as pl
from jax.experimental.pallas import tpu as pltpu
from jax.sharding import PartitionSpec as P


F32 = jnp.float32
BF16 = jnp.bfloat16
VMEM_LIMIT = 16 * 2**20


def send_order(cols, level):
    if level == 0:
        return sorted(range(1, cols), reverse=True)
    return list(range(1, cols))


def swap(value, axis, size, mask):
    return lax.ppermute(value, axis, [(i, i ^ mask) for i in range(size)])


def dot_t(a, b):
    return lax.dot_general(a, b, (((1,), (1,)), ((), ())), preferred_element_type=F32)


def dot_n(a, b):
    return lax.dot_general(a, b, (((1,), (0,)), ((), ())), preferred_element_type=F32)


def update(near, far, tile_refs, steps, repeat, cols):
    row = lax.axis_index("row")
    col = lax.axis_index("col")
    total = None
    for step, tile_ref in zip(steps, tile_refs):
        for group in range(repeat):
            place = row ^ ((col ^ step) + cols * group)
            odd = jnp.broadcast_to(place % 2, near.shape[1:]) == 1
            segment = jnp.where(odd, far[place // 2], near[place // 2])
            term = dot_t(segment, tile_ref[group])
            total = term if total is None else total + term
    return total


def pick(tile_refs, pair, group, first):
    even, odd = tile_refs[2 * pair], tile_refs[2 * pair + 1]
    odd_first = jnp.broadcast_to(first, even.shape[1:]) == 1
    return jnp.where(odd_first, odd[group], even[group])


def spread(solved, parity, tile_refs, repeat, out):
    cols = len(tile_refs)
    row = lax.axis_index("row")
    col = lax.axis_index("col")
    first = (row + col + parity) % 2
    for pair in range(cols // 2):
        for group in range(repeat):
            place = row ^ ((col ^ (2 * pair + first)) + cols * group)
            tile = pick(tile_refs, pair, group, first)
            out[place // 2] = dot_n(solved, tile).astype(out.dtype)


def first_kernel(rhs, dinv, out, out_b):
    solved = dot_t(rhs[0, 0], dinv[0, 0])
    out[...] = solved
    out_b[...] = solved.astype(BF16)


def pick_kernel(level, cols, pattern, raw, own):
    shape = own.shape[1:]
    for group in range(own.shape[0]):
        total = jnp.zeros(shape, F32)
        for slot in range(raw.shape[0]):
            place = jnp.broadcast_to(pattern[1, level, :, slot : slot + 1], shape)
            here = (place >= cols * group) & (place < cols * (group + 1))
            total = total + jnp.where(here, raw[slot].astype(F32), 0.0)
        own[group] = total.astype(BF16)


def early_kernel(repeat, cols, steps, near, far, *refs):
    refs[-1][...] = update(near, far, refs[:-1], steps, repeat, cols)


def forward_kernel(level, repeat, cols, steps, part, near, far, *refs):
    tile_refs, (rhs, dinv, out, out_b) = refs[: len(steps)], refs[len(steps) :]
    late = update(near, far, tile_refs, steps, repeat, cols)
    current = rhs[level, 0].astype(F32) - (part[...] + late)
    solved = dot_t(current.astype(BF16), dinv[level, 0])
    out[...] = solved
    out_b[...] = solved.astype(BF16)


def turn_kernel(level, repeat, cols, steps, part, near, far, *refs):
    tile_refs, (rhs, dinv, out, out_b, send) = refs[:cols], refs[cols:]
    late = update(near, far, [tile_refs[step] for step in steps], steps, repeat, cols)
    current = rhs[level, 0].astype(F32) - (part[...] + late)
    forward = dot_t(current.astype(BF16), dinv[level, 0])
    solved = dot_n(forward.astype(BF16), dinv[level, 0])
    out[...] = solved
    solved = solved.astype(BF16)
    out_b[...] = solved
    spread(solved, 1, tile_refs, repeat, send)


def keep_kernel(repeat, solved, *refs):
    spread(solved[...], 0, refs[:-1], repeat, refs[-1])


def remainder(count, refs):
    total = refs[0][...].astype(F32)
    for ref in refs[1:count]:
        total = total + ref[...].astype(F32)
    return total


def backward_kernel(level, repeat, cols, count, *refs):
    arrived, tile_refs = refs[:count], refs[count : count + cols]
    forward, dinv, out, out_b, send = refs[count + cols :]
    rest = forward[...] - remainder(count, arrived)
    solved = dot_n(rest.astype(BF16), dinv[level, 0])
    out[...] = solved
    solved = solved.astype(BF16)
    out_b[...] = solved
    spread(solved, 1, tile_refs, repeat, send)


def last_kernel(count, upper_count, *refs):
    arrived = refs[:count]
    forward, dinv = refs[count : count + 2]
    upper = refs[count + 2 : count + 2 + upper_count]
    out = refs[-1]
    rest = forward[...] - remainder(count, arrived)
    out[0, 0] = dot_n(rest.astype(BF16), dinv[0, 0])
    for index, ref in enumerate(upper):
        out[index + 1, 0] = ref[...]


def call(kernel, outs, scratch, *args):
    return pl.pallas_call(
        kernel,
        out_shape=outs,
        in_specs=[pl.BlockSpec(memory_space=pltpu.VMEM)] * len(args),
        out_specs=jax.tree.map(lambda _: pl.BlockSpec(memory_space=pltpu.VMEM), outs),
        scratch_shapes=scratch,
        compiler_params=pltpu.CompilerParams(vmem_limit_bytes=VMEM_LIMIT),
    )(*args)


def per_device(rhs, dinv, tiles, pattern):
    levels, blocks, nrhs, bs = rhs.shape
    assert blocks == 1
    cols = lax.axis_size("col")
    rows = lax.axis_size("row")
    repeat = rows // cols
    chips = rows // 2

    seg = jax.ShapeDtypeStruct((nrhs, bs), F32)
    seg_b = jax.ShapeDtypeStruct((nrhs, bs), BF16)
    chip_segs = jax.ShapeDtypeStruct((chips, nrhs, bs), F32)
    chip_segs_b = jax.ShapeDtypeStruct((chips, nrhs, bs), BF16)

    def gathered_tiles(level, after):
        source = tiles
        if after is not None:
            source, _ = lax.optimization_barrier((tiles, after))
        own = call(
            functools.partial(pick_kernel, level, cols),
            jax.ShapeDtypeStruct((repeat, bs, bs), BF16), [], pattern, source[level, 0],
        )
        found = [own] + [None] * (cols - 1)
        for step in send_order(cols, level):
            found[step] = swap(own, "col", cols, step)
        return found

    def gather(mine):
        near = [mine]
        for chip in range(1, chips):
            near.append(swap(mine, "row", rows, 2 * chip))
        near = jnp.stack(near)
        return near, swap(near, "row", rows, 1)

    def scatter(solved, send, found_tiles):
        other = swap(send, "row", rows, 1)
        keep = call(functools.partial(keep_kernel, repeat), chip_segs, [], solved, *found_tiles)
        total = keep + other.astype(F32)
        found = [total[0]]
        for chip in range(1, chips):
            found.append(swap(total[chip].astype(BF16), "row", rows, 2 * chip))
        return found

    late_steps = [send_order(cols, level)[-2:] for level in range(levels - 1)]

    def early_part(level, near, far, found_tiles):
        early_steps = [step for step in range(cols) if step not in late_steps[level - 1]]
        kernel = functools.partial(early_kernel, repeat, cols, early_steps)
        return call(kernel, seg, [], near, far, *[found_tiles[step] for step in early_steps])

    level_tiles = []
    for level in range(levels - 1):
        level_tiles.append(gathered_tiles(level, level_tiles[-1][0] if level_tiles else None))
    forward, mine = call(first_kernel, (seg, seg_b), [], rhs, dinv)
    forwards = [forward]
    for level in range(1, levels - 1):
        near, far = gather(mine)
        found_tiles = level_tiles[level - 1]
        forward, mine = call(
            functools.partial(forward_kernel, level, repeat, cols, late_steps[level - 1]),
            (seg, seg_b), [], early_part(level, near, far, found_tiles), near, far,
            *[found_tiles[step] for step in late_steps[level - 1]], rhs, dinv,
        )
        forwards.append(forward)
    top = levels - 1
    near, far = gather(mine)
    found_tiles = level_tiles[top - 1]
    solved, solved_b, send = call(
        functools.partial(turn_kernel, top, repeat, cols, late_steps[top - 1]),
        (seg, seg_b, chip_segs_b), [], early_part(top, near, far, found_tiles), near, far,
        *found_tiles, rhs, dinv,
    )
    upper = [solved]
    for level in range(levels - 2, 0, -1):
        arrived = scatter(solved_b, send, found_tiles)
        found_tiles = level_tiles[level - 1]
        solved, solved_b, send = call(
            functools.partial(backward_kernel, level, repeat, cols, chips),
            (seg, seg_b, chip_segs_b), [], *arrived, *found_tiles, forwards[level], dinv,
        )
        upper.insert(0, solved)
    arrived = scatter(solved_b, send, found_tiles)
    return call(
        functools.partial(last_kernel, chips, len(upper)),
        jax.ShapeDtypeStruct(rhs.shape, F32), [], *arrived, forwards[0], dinv, *upper,
    )


def solution(mesh):
    in_specs = (
        P(None, "row", None, None),
        P(None, "row", None, None),
        P(None, "row", "col", None, None),
        P(None, None, "row", "col"),
    )
    out_specs = P(None, "row", None, None)

    return jax.shard_map(
        per_device, mesh=mesh, in_specs=in_specs, out_specs=out_specs, check_vma=False
    )
```

```python
import functools

import jax
import jax.numpy as jnp
from jax import lax
from jax.experimental import pallas as pl
from jax.experimental.pallas import tpu as pltpu
from jax.sharding import PartitionSpec as P


F32 = jnp.float32
BF16 = jnp.bfloat16
VMEM_LIMIT = 16 * 2**20


def send_order(cols):
    return sorted(range(1, cols), key=lambda step: -step)


def swap(value, axis, size, mask):
    return lax.ppermute(value, axis, [(i, i ^ mask) for i in range(size)])


def dot_t(a, b):
    return lax.dot_general(a, b, (((1,), (1,)), ((), ())), preferred_element_type=F32)


def dot_n(a, b):
    return lax.dot_general(a, b, (((1,), (0,)), ((), ())), preferred_element_type=F32)


def update(near, far, tile_refs, steps, repeat, cols):
    row = lax.axis_index("row")
    col = lax.axis_index("col")
    total = None
    for step, tile_ref in zip(steps, tile_refs):
        for group in range(repeat):
            place = row ^ ((col ^ step) + cols * group)
            odd = jnp.broadcast_to(place % 2, near.shape[1:]) == 1
            segment = jnp.where(odd, far[place // 2], near[place // 2])
            term = dot_t(segment, tile_ref[group])
            total = term if total is None else total + term
    return total


def pick(tile_refs, pair, group, first):
    even, odd = tile_refs[2 * pair], tile_refs[2 * pair + 1]
    odd_first = jnp.broadcast_to(first, even.shape[1:]) == 1
    return jnp.where(odd_first, odd[group], even[group])


def spread(solved, parity, tile_refs, repeat, out):
    cols = len(tile_refs)
    row = lax.axis_index("row")
    col = lax.axis_index("col")
    first = (row + col + parity) % 2
    for pair in range(cols // 2):
        for group in range(repeat):
            place = row ^ ((col ^ (2 * pair + first)) + cols * group)
            tile = pick(tile_refs, pair, group, first)
            out[place // 2] = dot_n(solved, tile).astype(out.dtype)


def first_kernel(rhs, dinv, out, out_b):
    solved = dot_t(rhs[0, 0], dinv[0, 0])
    out[...] = solved
    out_b[...] = solved.astype(BF16)


def pick_kernel(level, cols, pattern, raw, own):
    shape = own.shape[1:]
    for group in range(own.shape[0]):
        total = jnp.zeros(shape, F32)
        for slot in range(raw.shape[0]):
            place = jnp.broadcast_to(pattern[1, level, :, slot : slot + 1], shape)
            here = (place >= cols * group) & (place < cols * (group + 1))
            total = total + jnp.where(here, raw[slot].astype(F32), 0.0)
        own[group] = total.astype(BF16)


def early_kernel(repeat, cols, steps, near, far, *refs):
    refs[-1][...] = update(near, far, refs[:-1], steps, repeat, cols)


def forward_kernel(level, repeat, cols, steps, part, near, far, *refs):
    tile_refs, (rhs, dinv, out, out_b) = refs[: len(steps)], refs[len(steps) :]
    late = update(near, far, tile_refs, steps, repeat, cols)
    current = rhs[level, 0].astype(F32) - (part[...] + late)
    solved = dot_t(current.astype(BF16), dinv[level, 0])
    out[...] = solved
    out_b[...] = solved.astype(BF16)


def turn_kernel(level, repeat, cols, steps, part, near, far, *refs):
    tile_refs, (rhs, dinv, out, out_b, send) = refs[:cols], refs[cols:]
    late = update(near, far, [tile_refs[step] for step in steps], steps, repeat, cols)
    current = rhs[level, 0].astype(F32) - (part[...] + late)
    forward = dot_t(current.astype(BF16), dinv[level, 0])
    solved = dot_n(forward.astype(BF16), dinv[level, 0])
    out[...] = solved
    solved = solved.astype(BF16)
    out_b[...] = solved
    spread(solved, 1, tile_refs, repeat, send)


def keep_kernel(repeat, solved, *refs):
    spread(solved[...], 0, refs[:-1], repeat, refs[-1])


def remainder(count, refs):
    total = refs[0][...].astype(F32)
    for ref in refs[1:count]:
        total = total + ref[...].astype(F32)
    return total


def backward_kernel(level, repeat, cols, count, *refs):
    arrived, tile_refs = refs[:count], refs[count : count + cols]
    forward, dinv, out, out_b, send = refs[count + cols :]
    rest = forward[...] - remainder(count, arrived)
    solved = dot_n(rest.astype(BF16), dinv[level, 0])
    out[...] = solved
    solved = solved.astype(BF16)
    out_b[...] = solved
    spread(solved, 1, tile_refs, repeat, send)


def last_kernel(count, upper_count, *refs):
    arrived = refs[:count]
    forward, dinv = refs[count : count + 2]
    upper = refs[count + 2 : count + 2 + upper_count]
    out, held, sems = refs[count + 2 + upper_count :]
    copies = [
        pltpu.make_async_copy(ref, out.at[index + 1, 0], sems.at[index + 1])
        for index, ref in enumerate(upper)
    ]
    for copy in copies:
        copy.start()
    rest = forward[...] - remainder(count, arrived)
    held[...] = dot_n(rest.astype(BF16), dinv[0, 0])
    final = pltpu.make_async_copy(held, out.at[0, 0], sems.at[0])
    final.start()
    for copy in copies:
        copy.wait()
    final.wait()


def call(kernel, outs, scratch, *args, out_space=pltpu.VMEM):
    return pl.pallas_call(
        kernel,
        out_shape=outs,
        in_specs=[pl.BlockSpec(memory_space=pltpu.VMEM)] * len(args),
        out_specs=jax.tree.map(lambda _: pl.BlockSpec(memory_space=out_space), outs),
        scratch_shapes=scratch,
        compiler_params=pltpu.CompilerParams(vmem_limit_bytes=VMEM_LIMIT),
    )(*args)


def per_device(rhs, dinv, tiles, pattern):
    levels, blocks, nrhs, bs = rhs.shape
    assert blocks == 1
    cols = lax.axis_size("col")
    rows = lax.axis_size("row")
    repeat = rows // cols
    chips = rows // 2

    seg = jax.ShapeDtypeStruct((nrhs, bs), F32)
    seg_b = jax.ShapeDtypeStruct((nrhs, bs), BF16)
    chip_segs = jax.ShapeDtypeStruct((chips, nrhs, bs), F32)
    chip_segs_b = jax.ShapeDtypeStruct((chips, nrhs, bs), BF16)

    def gathered_tiles(level, after):
        source = tiles
        if after is not None:
            source, _ = lax.optimization_barrier((tiles, after))
        own = call(
            functools.partial(pick_kernel, level, cols),
            jax.ShapeDtypeStruct((repeat, bs, bs), BF16), [], pattern, source[level, 0],
        )
        found = [own] + [None] * (cols - 1)
        for step in send_order(cols):
            found[step] = swap(own, "col", cols, step)
        return found

    def gather(mine):
        near = [mine]
        for chip in range(1, chips):
            near.append(swap(mine, "row", rows, 2 * chip))
        near = jnp.stack(near)
        return near, swap(near, "row", rows, 1)

    def scatter(solved, send, found_tiles):
        other = swap(send, "row", rows, 1)
        keep = call(functools.partial(keep_kernel, repeat), chip_segs, [], solved, *found_tiles)
        total = keep + other.astype(F32)
        found = [total[0]]
        for chip in range(1, chips):
            found.append(swap(total[chip].astype(BF16), "row", rows, 2 * chip))
        return found

    late_steps = send_order(cols)[-2:]
    early_steps = [step for step in range(cols) if step not in late_steps]

    def early_part(near, far, found_tiles):
        kernel = functools.partial(early_kernel, repeat, cols, early_steps)
        return call(kernel, seg, [], near, far, *[found_tiles[step] for step in early_steps])

    level_tiles = []
    for level in range(levels - 1):
        level_tiles.append(gathered_tiles(level, level_tiles[-1][0] if level_tiles else None))
    forward, mine = call(first_kernel, (seg, seg_b), [], rhs, dinv)
    forwards = [forward]
    for level in range(1, levels - 1):
        near, far = gather(mine)
        found_tiles = level_tiles[level - 1]
        forward, mine = call(
            functools.partial(forward_kernel, level, repeat, cols, late_steps),
            (seg, seg_b), [], early_part(near, far, found_tiles), near, far,
            *[found_tiles[step] for step in late_steps], rhs, dinv,
        )
        forwards.append(forward)
    top = levels - 1
    near, far = gather(mine)
    found_tiles = level_tiles[top - 1]
    solved, solved_b, send = call(
        functools.partial(turn_kernel, top, repeat, cols, late_steps),
        (seg, seg_b, chip_segs_b), [], early_part(near, far, found_tiles), near, far,
        *found_tiles, rhs, dinv,
    )
    upper = [solved]
    for level in range(levels - 2, 0, -1):
        arrived = scatter(solved_b, send, found_tiles)
        found_tiles = level_tiles[level - 1]
        solved, solved_b, send = call(
            functools.partial(backward_kernel, level, repeat, cols, chips),
            (seg, seg_b, chip_segs_b), [], *arrived, *found_tiles, forwards[level], dinv,
        )
        upper.insert(0, solved)
    arrived = scatter(solved_b, send, found_tiles)
    return call(
        functools.partial(last_kernel, chips, len(upper)),
        jax.ShapeDtypeStruct(rhs.shape, F32),
        [pltpu.VMEM((nrhs, bs), F32), pltpu.SemaphoreType.DMA((levels,))],
        *arrived, forwards[0], dinv, *upper, out_space=pl.ANY,
    )


def solution(mesh):
    in_specs = (
        P(None, "row", None, None),
        P(None, "row", None, None),
        P(None, "row", "col", None, None),
        P(None, None, "row", "col"),
    )
    out_specs = P(None, "row", None, None)

    return jax.shard_map(
        per_device, mesh=mesh, in_specs=in_specs, out_specs=out_specs, check_vma=False
    )
```

```python
import functools

import jax
import jax.numpy as jnp
from jax import lax
from jax.experimental import pallas as pl
from jax.experimental.pallas import tpu as pltpu
from jax.sharding import PartitionSpec as P


F32 = jnp.float32
BF16 = jnp.bfloat16
VMEM_LIMIT = 16 * 2**20


def send_order(cols):
    return sorted(range(1, cols), key=lambda step: -step)


def swap(value, axis, size, mask):
    return lax.ppermute(value, axis, [(i, i ^ mask) for i in range(size)])


def dot_t(a, b):
    return lax.dot_general(a, b, (((1,), (1,)), ((), ())), preferred_element_type=F32)


def dot_n(a, b):
    return lax.dot_general(a, b, (((1,), (0,)), ((), ())), preferred_element_type=F32)


def update(near, far, tile_refs, steps, repeat, cols):
    row = lax.axis_index("row")
    col = lax.axis_index("col")
    total = None
    for step, tile_ref in zip(steps, tile_refs):
        for group in range(repeat):
            place = row ^ ((col ^ step) + cols * group)
            odd = jnp.broadcast_to(place % 2, near.shape[1:]) == 1
            segment = jnp.where(odd, far[place // 2], near[place // 2])
            term = dot_t(segment, tile_ref[group])
            total = term if total is None else total + term
    return total


def pick(tile_refs, pair, group, first):
    even, odd = tile_refs[2 * pair], tile_refs[2 * pair + 1]
    odd_first = jnp.broadcast_to(first, even.shape[1:]) == 1
    return jnp.where(odd_first, odd[group], even[group])


def spread(solved, parity, tile_refs, repeat, out):
    cols = len(tile_refs)
    row = lax.axis_index("row")
    col = lax.axis_index("col")
    first = (row + col + parity) % 2
    for pair in range(cols // 2):
        for group in range(repeat):
            place = row ^ ((col ^ (2 * pair + first)) + cols * group)
            tile = pick(tile_refs, pair, group, first)
            out[place // 2] = dot_n(solved, tile).astype(out.dtype)


def first_kernel(rhs, dinv, out, out_b):
    solved = dot_t(rhs[0, 0], dinv[0, 0])
    out[...] = solved
    out_b[...] = solved.astype(BF16)


def pick_kernel(level, cols, pattern, raw, own):
    shape = own.shape[1:]
    for group in range(own.shape[0]):
        total = jnp.zeros(shape, F32)
        for slot in range(raw.shape[0]):
            place = jnp.broadcast_to(pattern[1, level, :, slot : slot + 1], shape)
            here = (place >= cols * group) & (place < cols * (group + 1))
            total = total + jnp.where(here, raw[slot].astype(F32), 0.0)
        own[group] = total.astype(BF16)


def early_kernel(repeat, cols, steps, near, far, *refs):
    refs[-1][...] = update(near, far, refs[:-1], steps, repeat, cols)


def forward_kernel(level, repeat, cols, steps, part, near, far, *refs):
    tile_refs, (rhs, dinv, out, out_b) = refs[: len(steps)], refs[len(steps) :]
    late = update(near, far, tile_refs, steps, repeat, cols)
    current = rhs[level, 0].astype(F32) - (part[...] + late)
    solved = dot_t(current.astype(BF16), dinv[level, 0])
    out[...] = solved
    out_b[...] = solved.astype(BF16)


def turn_kernel(level, repeat, cols, steps, part, near, far, *refs):
    tile_refs, (rhs, dinv, out, out_b, send) = refs[:cols], refs[cols:]
    late = update(near, far, [tile_refs[step] for step in steps], steps, repeat, cols)
    current = rhs[level, 0].astype(F32) - (part[...] + late)
    forward = dot_t(current.astype(BF16), dinv[level, 0])
    solved = dot_n(forward.astype(BF16), dinv[level, 0])
    out[...] = solved
    solved = solved.astype(BF16)
    out_b[...] = solved
    spread(solved, 1, tile_refs, repeat, send)


def keep_kernel(repeat, solved, *refs):
    spread(solved[...], 0, refs[:-1], repeat, refs[-1])


def remainder(count, refs):
    total = refs[0][...].astype(F32)
    for ref in refs[1:count]:
        total = total + ref[...].astype(F32)
    return total


def backward_kernel(level, repeat, cols, count, *refs):
    arrived, tile_refs = refs[:count], refs[count : count + cols]
    forward, dinv, out, out_b, send = refs[count + cols :]
    rest = forward[...] - remainder(count, arrived)
    solved = dot_n(rest.astype(BF16), dinv[level, 0])
    out[...] = solved
    solved = solved.astype(BF16)
    out_b[...] = solved
    spread(solved, 1, tile_refs, repeat, send)


def last_kernel(count, upper_count, *refs):
    arrived = refs[:count]
    forward, dinv = refs[count : count + 2]
    upper = refs[count + 2 : count + 2 + upper_count]
    out = refs[-1]
    rest = forward[...] - remainder(count, arrived)
    out[0, 0] = dot_n(rest.astype(BF16), dinv[0, 0])
    for index, ref in enumerate(upper):
        out[index + 1, 0] = ref[...]


def call(kernel, outs, scratch, *args):
    return pl.pallas_call(
        kernel,
        out_shape=outs,
        in_specs=[pl.BlockSpec(memory_space=pltpu.VMEM)] * len(args),
        out_specs=jax.tree.map(lambda _: pl.BlockSpec(memory_space=pltpu.VMEM), outs),
        scratch_shapes=scratch,
        compiler_params=pltpu.CompilerParams(vmem_limit_bytes=VMEM_LIMIT),
    )(*args)


def per_device(rhs, dinv, tiles, pattern):
    levels, blocks, nrhs, bs = rhs.shape
    assert blocks == 1
    cols = lax.axis_size("col")
    rows = lax.axis_size("row")
    repeat = rows // cols
    chips = rows // 2

    seg = jax.ShapeDtypeStruct((nrhs, bs), F32)
    seg_b = jax.ShapeDtypeStruct((nrhs, bs), BF16)
    chip_segs = jax.ShapeDtypeStruct((chips, nrhs, bs), F32)
    chip_segs_b = jax.ShapeDtypeStruct((chips, nrhs, bs), BF16)

    def gathered_tiles(level, after):
        source = tiles
        if after is not None:
            source, _ = lax.optimization_barrier((tiles, after))
        own = call(
            functools.partial(pick_kernel, level, cols),
            jax.ShapeDtypeStruct((repeat, bs, bs), BF16), [], pattern, source[level, 0],
        )
        found = [own] + [None] * (cols - 1)
        for step in send_order(cols):
            found[step] = swap(own, "col", cols, step)
        return found

    def gather(mine):
        near = [mine]
        for chip in range(1, chips):
            near.append(swap(mine, "row", rows, 2 * chip))
        near = jnp.stack(near)
        return near, swap(near, "row", rows, 1)

    def scatter(solved, send, found_tiles):
        other = swap(send, "row", rows, 1)
        keep = call(functools.partial(keep_kernel, repeat), chip_segs, [], solved, *found_tiles)
        total = keep + other.astype(F32)
        found = [total[0]]
        for chip in range(1, chips):
            found.append(swap(total[chip].astype(BF16), "row", rows, 2 * chip))
        return found

    late_steps = send_order(cols)[-2:]
    early_steps = [step for step in range(cols) if step not in late_steps]

    def early_part(near, far, found_tiles):
        kernel = functools.partial(early_kernel, repeat, cols, early_steps)
        return call(kernel, seg, [], near, far, *[found_tiles[step] for step in early_steps])

    level_tiles = []
    for level in range(levels - 1):
        level_tiles.append(gathered_tiles(level, level_tiles[-1][0] if level_tiles else None))
    forward, mine = call(first_kernel, (seg, seg_b), [], rhs, dinv)
    forwards = [forward]
    for level in range(1, levels - 1):
        near, far = gather(mine)
        found_tiles = level_tiles[level - 1]
        forward, mine = call(
            functools.partial(forward_kernel, level, repeat, cols, late_steps),
            (seg, seg_b), [], early_part(near, far, found_tiles), near, far,
            *[found_tiles[step] for step in late_steps], rhs, dinv,
        )
        forwards.append(forward)
    top = levels - 1
    near, far = gather(mine)
    found_tiles = level_tiles[top - 1]
    solved, solved_b, send = call(
        functools.partial(turn_kernel, top, repeat, cols, late_steps),
        (seg, seg_b, chip_segs_b), [], early_part(near, far, found_tiles), near, far,
        *found_tiles, rhs, dinv,
    )
    upper = [solved]
    for level in range(levels - 2, 0, -1):
        arrived = scatter(solved_b, send, found_tiles)
        found_tiles = level_tiles[level - 1]
        solved, solved_b, send = call(
            functools.partial(backward_kernel, level, repeat, cols, chips),
            (seg, seg_b, chip_segs_b), [], *arrived, *found_tiles, forwards[level], dinv,
        )
        upper.insert(0, solved)
    arrived = scatter(solved_b, send, found_tiles)
    return call(
        functools.partial(last_kernel, chips, len(upper)),
        jax.ShapeDtypeStruct(rhs.shape, F32), [], *arrived, forwards[0], dinv, *upper,
    )


def solution(mesh):
    in_specs = (
        P(None, "row", None, None),
        P(None, "row", None, None),
        P(None, "row", "col", None, None),
        P(None, None, "row", "col"),
    )
    out_specs = P(None, "row", None, None)

    return jax.shard_map(
        per_device, mesh=mesh, in_specs=in_specs, out_specs=out_specs, check_vma=False
    )
```
